128 devices in a mesh: dp: 2 (over x_hi), pipe: 4 (over z), tensor: 16 (over x_lo, y, core).
Axes of the slice: x: 4 (x_hi: 2, x_lo: 2; x = x_hi * 2 + x_lo), y: 4, z: 4, core: 2. Of those that a mesh axis runs over, the one named last changes fastest.
Arguments:
- inputs: bfloat16 [4, 3072, 8192], P('pipe', 'dp', 'tensor'), may hold values from -6 to 6
- upstream: bfloat16 [4, 3072, 8192], P('pipe', 'dp', 'tensor'), may hold values from -6 to 6
- factor_one: bfloat16 [4, 32, 4, 256, 256], P('pipe', 'tensor'), may hold values from -0.375 to 0.375
- factor_two: bfloat16 [4, 128, 256, 256], P('pipe', 'tensor'), may hold values from -0.375 to 0.375
- factor_three: bfloat16 [4, 128, 256, 256], P('pipe', 'tensor'), may hold values from -0.375 to 0.375
- factor_four: bfloat16 [4, 32, 4, 256, 256], P('pipe', 'tensor'), may hold values from -0.1875 to 0.1875
Outputs:
- y_next: bfloat16 [4, 3072, 8192], P('pipe', 'dp', 'tensor')
- dx_prev: bfloat16 [4, 3072, 8192], P('pipe', 'dp', 'tensor')
- grad_one: float32 [4, 32, 4, 256, 256], P('pipe', 'tensor')
- grad_two: float32 [4, 128, 256, 256], P('pipe', 'tensor')
- grad_three: float32 [4, 128, 256, 256], P('pipe', 'tensor')
- grad_four: float32 [4, 32, 4, 256, 256], P('pipe', 'tensor')
The draws below stay inside these ranges and needn't reach their ends.
All inputs are finite; a program needn't handle non-finite values.
Results may differ from the reference program's by a relative error of at most 0.0068.
Values may be sent and summed in bfloat16 or wider, within the bound.
No kernel may reach another device: no remote copies, remote signals or barrier semaphores. Data moves between devices by JAX's collectives and lax.ppermute only.
A program may use at most 192 MiB of HBM per device.

```python
import jax
import jax.numpy as jnp
from jax import lax

D = 8192
BS = 256
SECTIONS = 4
TOKENS = 3072
NG = 32
NM = 128
EXPAND = 4


def steps_of(key, extent, split, smallest, top_value):
    def one(axis_at, blocks):
        draws = jax.random.uniform(jax.random.fold_in(jax.random.fold_in(key, 6), axis_at), (blocks,), jnp.float32, smallest / len(split), top_value / len(split))
        return jnp.repeat(jnp.exp(draws), extent[axis_at] // blocks).reshape((-1,) + (1,) * (len(extent) - axis_at - 1))

    factor_of = one(*split[0])
    for cut in split[1:]:
        factor_of = factor_of * one(*cut)
    return factor_of


def normal_values(own_key, dims, scale, most, shards=(), held_as=jnp.bfloat16):
    entries = jax.random.normal(own_key, dims, jnp.float32) * scale
    if len(shards) > 0:
        entries = steps_of(own_key, dims, shards, -0.22, 0.18) * entries
    return jnp.clip(entries, min=-most, max=most).astype(held_as)


def setup_inputs(seed: int = 0) -> dict:
    arg_keys = jax.random.split(jax.random.key(seed), 7)
    inputs = normal_values(arg_keys[0], (SECTIONS, TOKENS, D), 1.0, 6.0, ((0, 4), (1, 2), (2, 16)))
    upstream = normal_values(arg_keys[1], (SECTIONS, TOKENS, D), 1.0, 6.0, ((0, 4), (1, 2), (2, 16)))
    factor_one = normal_values(arg_keys[2], (SECTIONS, NG, EXPAND, BS, BS), BS ** -0.5, 0.375, ((0, 4), (1, 16)))
    factor_two = normal_values(arg_keys[3], (SECTIONS, NM, BS, BS), BS ** -0.5, 0.375, ((0, 4), (1, 16)))
    factor_three = normal_values(arg_keys[4], (SECTIONS, NM, BS, BS), BS ** -0.5, 0.375, ((0, 4), (1, 16)))
    factor_four = normal_values(arg_keys[5], (SECTIONS, NG, EXPAND, BS, BS), (EXPAND * BS) ** -0.5, 0.1875, ((0, 4), (1, 16)))
    return {"inputs": inputs, "upstream": upstream, "factor_one": factor_one, "factor_two": factor_two, "factor_three": factor_three, "factor_four": factor_four}


def permute(blocks):
    rows, count, width = blocks.shape
    inner = width // count
    return blocks.reshape(rows, count, count, inner).transpose(0, 2, 1, 3).reshape(rows, count, width)

def one_section(operands):
    acts, grad_out, factor_one, factor_two, factor_three, factor_four = operands
    groups, expand, bsize = (factor_one.shape[0], factor_one.shape[1], factor_one.shape[2])
    rows = acts.shape[0]
    one_f = factor_one.astype(jnp.float32)
    two_f = factor_two.astype(jnp.float32)
    three_f = factor_three.astype(jnp.float32)
    four_f = factor_four.astype(jnp.float32)
    grouped = acts.reshape(rows, groups, bsize).astype(jnp.float32)
    lifted = jnp.einsum('tgi,gkij->tgkj', grouped, one_f).astype(jnp.bfloat16).reshape(rows, groups * expand, bsize)
    mixed = permute(lifted)
    preact = jnp.einsum('tcj,cjn->tcn', mixed.astype(jnp.float32), two_f)
    active = jax.nn.gelu(preact).astype(jnp.bfloat16)
    narrowed = jnp.einsum('tcn,cno->tco', active.astype(jnp.float32), three_f).astype(jnp.bfloat16)
    spread = permute(narrowed)
    spread_four = spread.reshape(rows, groups, expand, bsize).astype(jnp.float32)
    output = jnp.einsum('tgkr,gkro->tgo', spread_four, four_f).astype(jnp.bfloat16).reshape(rows, groups * bsize)
    grad_grouped = grad_out.reshape(rows, groups, bsize).astype(jnp.float32)
    grad_spread = jnp.einsum('tgo,gkro->tgkr', grad_grouped, four_f).astype(jnp.bfloat16).reshape(rows, groups * expand, bsize)
    grad_four = jnp.einsum('tgkr,tgo->gkro', spread_four, grad_grouped)
    grad_narrow = permute(grad_spread)
    grad_active = jnp.einsum('tco,cno->tcn', grad_narrow.astype(jnp.float32), three_f)
    grad_three = jnp.einsum('tcn,tco->cno', active.astype(jnp.float32), grad_narrow.astype(jnp.float32))
    pulled = jax.vjp(jax.nn.gelu, preact)[1]
    grad_pre = pulled(grad_active)[0].astype(jnp.bfloat16)
    grad_two = jnp.einsum('tcj,tcn->cjn', mixed.astype(jnp.float32), grad_pre.astype(jnp.float32))
    grad_mixed = jnp.einsum('tcn,cjn->tcj', grad_pre.astype(jnp.float32), two_f).astype(jnp.bfloat16)
    grad_lift = permute(grad_mixed)
    lift_four = grad_lift.reshape(rows, groups, expand, bsize).astype(jnp.float32)
    grad_input = jnp.einsum('tgkj,gkij->tgi', lift_four, one_f).astype(jnp.bfloat16).reshape(rows, groups * bsize)
    grad_one = jnp.einsum('tgi,tgkj->gkij', grouped, lift_four)
    return (output, grad_input, grad_one, grad_two, grad_three, grad_four)

def reference(inputs, upstream, factor_one, factor_two, factor_three, factor_four):
    output, grad_input, grad_one, grad_two, grad_three, grad_four = lax.map(one_section, (inputs, upstream, factor_one, factor_two, factor_three, factor_four))
    y_next = jnp.concatenate([jnp.zeros_like(output[:1]), output[:-1]], axis=0)
    dx_prev = jnp.concatenate([grad_input[1:], jnp.zeros_like(grad_input[:1])], axis=0)
    return (y_next, dx_prev, grad_one, grad_two, grad_three, grad_four)
```

```python
import functools
import math

import jax
import jax.numpy as jnp
from jax import lax
from jax.experimental import pallas as pl
from jax.experimental.pallas import tpu as pltpu
from jax.sharding import Mesh, PartitionSpec as P

BF = jnp.bfloat16
F32 = jnp.float32
GELU_A = math.sqrt(2.0 / math.pi)
GELU_B = 0.044715
YC = ("y", "core")


def params(mib):
    return pltpu.CompilerParams(vmem_limit_bytes=mib * 1024 * 1024)


def cost(flops, nbytes, trans=0):
    return pl.CostEstimate(flops=int(flops), bytes_accessed=int(nbytes), transcendentals=int(trans))


def mm(a, b, dims):
    return lax.dot_general(a, b, (dims, ((), ())), preferred_element_type=F32)


def one_hot(shape, row_dim, group, k, sub):
    row = lax.broadcasted_iota(jnp.int32, shape, row_dim)
    col = lax.broadcasted_iota(jnp.int32, shape, 1 - row_dim)
    per = sub // 2
    first = group * per + k * 2
    inside = row % sub
    hit = ((row // sub) == (col // 2)) & (inside == first + col % 2)
    return jnp.where(hit, 1.0, 0.0).astype(BF)


def lift_body(swap, side_ref, x_ref, f_ref, out_ref, a_ref):
    groups, expand = f_ref.shape[0], f_ref.shape[1]
    rows, width = a_ref.shape
    wide = width // groups
    sub = groups * expand * 2
    cols = 2 * rows // sub

    @pl.when(pl.program_id(0) == 0)
    def _():
        for g in range(groups):
            total = jnp.zeros((rows, wide), F32)
            for k in range(expand):
                pick = one_hot((rows, cols), 0, g, k, sub)
                total += mm(pick, f_ref[g, k], ((1,), (1,)) if swap else ((1,), (0,)))
            a_ref[:, g * wide : (g + 1) * wide] = total.astype(BF)

    value = mm(a_ref[...], x_ref[...], ((1,), (1,))).astype(BF)
    out_ref[...] = value.reshape(out_ref.shape)


def lift(x, factor, side, peers, swap, tile):
    tokens, width = x.shape
    groups, expand, bsize = factor.shape[0], factor.shape[1], factor.shape[2 if swap else 3]
    local = groups * expand
    rows = peers * local * local * 2
    cols = peers * local * 2
    if swap:
        block, where = (groups, expand, bsize, cols), lambda i, s: (0, 0, 0, s[0])
    else:
        block, where = (groups, expand, cols, bsize), lambda i, s: (0, 0, s[0], 0)
    return pl.pallas_call(
        functools.partial(lift_body, swap),
        grid_spec=pltpu.PrefetchScalarGridSpec(
            num_scalar_prefetch=1,
            grid=(tokens // tile,),
            in_specs=[
                pl.BlockSpec((tile, width), lambda i, s: (i, 0)),
                pl.BlockSpec(block, where),
            ],
            out_specs=[
                pl.BlockSpec((peers, rows // peers, tile), lambda i, s: (0, 0, i)),
                pl.BlockSpec((rows, width), lambda i, s: (0, 0)),
            ],
        ),
        out_shape=[
            jax.ShapeDtypeStruct((peers, rows // peers, tokens), BF),
            jax.ShapeDtypeStruct((rows, width), BF),
        ],
        compiler_params=params(40),
        cost_estimate=cost(4 * rows * width * tokens, 2 * tokens * (width + rows)),
        name="lift",
    )(side, x, factor)


def gather_rows(scratch, side, own, peer):
    half = scratch.shape[0] // 2
    mine = pl.multiple_of(side * half, half)
    theirs = pl.multiple_of((1 - side) * half, half)
    scratch[pl.ds(mine, half), :] = own[...].reshape(half, scratch.shape[1])
    scratch[pl.ds(theirs, half), :] = peer[...].reshape(half, scratch.shape[1])


def split_rows(scratch, side, own, peer):
    half = scratch.shape[0] // 2
    mine = pl.multiple_of(side * half, half)
    theirs = pl.multiple_of((1 - side) * half, half)
    own[...] = scratch[pl.ds(mine, half), :].reshape(own.shape)
    peer[...] = scratch[pl.ds(theirs, half), :].reshape(peer.shape)


def forward_body(side_ref, ro_ref, rp_ref, w2_ref, w3_ref, no_ref, np_ref, mixed, narrow):
    side = side_ref[0]
    gather_rows(mixed, side, ro_ref, rp_ref)
    pre = mm(w2_ref[0], mixed[...], ((0,), (0,)))
    act = (0.5 * pre * (1.0 + jnp.tanh(GELU_A * (pre + GELU_B * (pre * pre * pre))))).astype(BF)
    narrow[...] = mm(w3_ref[0], act, ((0,), (0,))).astype(BF)
    split_rows(narrow, side, no_ref, np_ref)


def middle_specs(peers, local, sub, bsize, tile):
    piece = pl.BlockSpec((peers, 1, sub, tile), lambda c, i, s: (0, c, 0, i))
    weight = pl.BlockSpec((1, bsize, bsize), lambda c, i, s: (c, 0, 0))
    return piece, weight


def forward(side, own, peer, second, third, tile):
    peers, local, sub, tokens = own.shape
    bsize = second.shape[1]
    piece, weight = middle_specs(peers, local, sub, bsize, tile)
    shape = jax.ShapeDtypeStruct(own.shape, BF)
    return pl.pallas_call(
        forward_body,
        grid_spec=pltpu.PrefetchScalarGridSpec(
            num_scalar_prefetch=1,
            grid=(local, tokens // tile),
            in_specs=[piece, piece, weight, weight],
            out_specs=[piece, piece],
            scratch_shapes=[pltpu.VMEM((bsize, tile), BF), pltpu.VMEM((bsize, tile), BF)],
        ),
        out_shape=[shape, shape],
        compiler_params=params(32),
        cost_estimate=cost(
            4 * local * bsize * bsize * tokens, 4 * local * bsize * tokens, local * bsize * tokens
        ),
        name="forward",
    )(side, own, peer, second, third)


def backward_body(
    side_ref, ro_ref, rp_ref, go_ref, gp_ref, w2_ref, w3_ref,
    mo_ref, mp_ref, g2_ref, g3_ref, mixed, gnar, gmix, acc2, acc3,
):
    side = side_ref[0]
    step = pl.program_id(1)
    gather_rows(mixed, side, ro_ref, rp_ref)
    gather_rows(gnar, side, go_ref, gp_ref)
    pre = mm(w2_ref[0], mixed[...], ((0,), (0,)))
    square = pre * pre
    th = jnp.tanh(GELU_A * (pre + GELU_B * (square * pre)))
    half = 0.5 * (1.0 + th)
    act = (pre * half).astype(BF)
    slope = half + (0.5 * GELU_A) * pre * (1.0 - th * th) * (1.0 + (3.0 * GELU_B) * square)
    grad_act = mm(w3_ref[0], gnar[...], ((1,), (0,)))
    grad_pre = (grad_act * slope).astype(BF)
    gmix[...] = mm(w2_ref[0], grad_pre, ((1,), (0,))).astype(BF)
    split_rows(gmix, side, mo_ref, mp_ref)
    add3 = mm(act, gnar[...], ((1,), (1,)))
    add2 = mm(mixed[...], grad_pre, ((1,), (1,)))

    @pl.when(step == 0)
    def _():
        acc2[...] = add2
        acc3[...] = add3

    @pl.when(step > 0)
    def _():
        acc2[...] += add2
        acc3[...] += add3

    @pl.when(step == pl.num_programs(1) - 1)
    def _():
        g2_ref[0] = acc2[...].astype(BF)
        g3_ref[0] = acc3[...].astype(BF)


def backward(side, own, peer, grad_own, grad_peer, second, third, tile):
    peers, local, sub, tokens = own.shape
    bsize = second.shape[1]
    piece, weight = middle_specs(peers, local, sub, bsize, tile)
    shape = jax.ShapeDtypeStruct(own.shape, BF)
    grads = jax.ShapeDtypeStruct(second.shape, BF)
    return pl.pallas_call(
        backward_body,
        grid_spec=pltpu.PrefetchScalarGridSpec(
            num_scalar_prefetch=1,
            grid=(local, tokens // tile),
            in_specs=[piece] * 4 + [weight] * 2,
            out_specs=[piece, piece, weight, weight],
            scratch_shapes=[pltpu.VMEM((bsize, tile), BF)] * 3
            + [pltpu.VMEM((bsize, bsize), F32)] * 2,
        ),
        out_shape=[shape, shape, grads, grads],
        compiler_params=params(40),
        cost_estimate=cost(
            10 * local * bsize * bsize * tokens, 6 * local * bsize * tokens, local * bsize * tokens
        ),
        name="backward",
    )(side, own, peer, grad_own, grad_peer, second, third)


def drop_body(swap, add, groups, expand, s_ref, a_ref, x_ref, *rest):
    if add:
        prev_ref, out_ref, g_ref, flip, acc = rest
    else:
        out_ref, g_ref, flip, acc = rest
    step = pl.program_id(0)
    rows, width = a_ref.shape
    wide = width // groups
    sub = groups * expand * 2
    cols = 2 * rows // sub

    @pl.when(step == 0)
    def _():
        flip[...] = a_ref[...].T

    value = mm(flip[...], s_ref[...], ((1,), (0,))).T
    if add:
        value = value + prev_ref[...].astype(F32)
    out_ref[...] = value.astype(BF)
    more = mm(s_ref[...], x_ref[...], ((1,), (0,)))

    @pl.when(step == 0)
    def _():
        acc[...] = more

    @pl.when(step > 0)
    def _():
        acc[...] += more

    @pl.when(step == pl.num_programs(0) - 1)
    def _():
        for g in range(groups):
            part = acc[:, g * wide : (g + 1) * wide].astype(BF)
            if swap:
                part = part.T
            for k in range(expand):
                if swap:
                    got = mm(part, one_hot((rows, cols), 0, g, k, sub), ((1,), (0,)))
                else:
                    got = mm(one_hot((cols, rows), 1, g, k, sub), part, ((1,), (0,)))
                g_ref[g, k] = got.astype(BF)


def drop(s, a, x, prev, groups, expand, swap, tile):
    rows, width = a.shape
    tokens = x.shape[0]
    bsize = width // groups
    cols = rows // (groups * expand)
    grads = (groups, expand, bsize, cols) if swap else (groups, expand, cols, bsize)
    add = prev is not None
    wide = pl.BlockSpec((tile, width), lambda i: (i, 0))
    args = (s, a, x) + ((prev,) if add else ())
    return pl.pallas_call(
        functools.partial(drop_body, swap, add, groups, expand),
        grid=(tokens // tile,),
        in_specs=[
            pl.BlockSpec((rows, tile), lambda i: (0, i)),
            pl.BlockSpec((rows, width), lambda i: (0, 0)),
            wide,
        ]
        + ([wide] if add else []),
        out_specs=[wide, pl.BlockSpec(grads, lambda i: (0, 0, 0, 0))],
        scratch_shapes=[pltpu.VMEM((width, rows), BF), pltpu.VMEM((rows, width), F32)],
        out_shape=[
            jax.ShapeDtypeStruct((tokens, width), BF),
            jax.ShapeDtypeStruct(grads, BF),
        ],
        compiler_params=params(40),
        cost_estimate=cost(4 * rows * width * tokens, 2 * tokens * (rows + 3 * width)),
        name="drop",
    )(*args)


def swapped(value, axes):
    count = lax.axis_size(axes)
    return lax.ppermute(value, axes, [(i, count - 1 - i) for i in range(count)])


def shifted(value, axis, steps):
    count = lax.axis_size(axis)
    leading, last = (max(0, -steps), min(count, count - steps))
    return lax.ppermute(value, axis, [(source, source + steps) for source in range(leading, last)])


def spread_out(value):
    return lax.all_to_all(value, YC, split_axis=0, concat_axis=0, tiled=True)


def halves(value, dim):
    size = value.shape[dim] // 2
    return lax.slice_in_dim(value, 0, size, axis=dim), lax.slice_in_dim(value, size, 2 * size, axis=dim)


def paired(own, peer, axis_dim, is_low):
    mine = own.astype(F32) + swapped(own, "dp").astype(F32)
    theirs = swapped(peer, "xlo").astype(F32) + swapped(peer, ("dp", "xlo")).astype(F32)
    low = jnp.where(is_low, mine, theirs)
    high = jnp.where(is_low, theirs, mine)
    return jnp.concatenate([low, high], axis=axis_dim)


def shards(inputs, upstream, factor_one, factor_two, factor_three, factor_four):
    x, u = inputs[0], upstream[0]
    first, second, third, fourth = factor_one[0], factor_two[0], factor_three[0], factor_four[0]
    groups, expand, bsize = first.shape[0], first.shape[1], first.shape[2]
    local = groups * expand
    tokens = x.shape[0]
    peers = lax.axis_size("y") * lax.axis_size("core")
    place = lax.axis_index("xlo")
    is_low = place == 0
    side = place.astype(jnp.int32).reshape(1)
    zero = jnp.zeros((1,), jnp.int32)
    tile = 512 if tokens % 512 == 0 else tokens

    low, high = halves(first, 3)
    first_peer = swapped(jnp.where(is_low, high, low), "xlo")
    low, high = halves(fourth, 2)
    fourth_peer = swapped(jnp.where(is_low, high, low), "xlo")
    x_peer = swapped(x, "xlo")
    u_peer = swapped(u, "xlo")

    l1o, a1o = lift(x, first, side, peers, True, tile)
    l2o, a4o = lift(u, fourth, side, peers, False, tile)
    l1p, a1p = lift(x_peer, first_peer, zero, peers, True, tile)
    l2p, a4p = lift(u_peer, fourth_peer, zero, peers, False, tile)

    def inner(value):
        return spread_out(value).reshape(peers, local, 2 * local, tokens)

    def outer(value):
        return spread_out(value.reshape(peers, 2 * local * local, tokens)).reshape(-1, tokens)

    y1o = inner(l1o)
    y2o = inner(l2o)
    y1p = inner(l1p)
    y2p = inner(l2p)
    no, np_ = forward(side, y1o, y1p, second, third, tile)
    y3p = outer(np_)
    y3o = outer(no)
    mo, mp, g2, g3 = backward(side, y1o, y1p, y2o, y2p, second, third, tile)
    y4p = outer(mp)
    y4o = outer(mo)

    out_p, g4p = drop(y3p, a4p, u_peer, None, groups, expand, False, tile)
    out_o, g4o = drop(y3o, a4o, u, swapped(out_p, "xlo"), groups, expand, False, tile)
    y_next = shifted(out_o, "pipe", 1)
    in_p, g1p = drop(y4p, a1p, x_peer, None, groups, expand, True, tile)
    in_o, g1o = drop(y4o, a1o, x, swapped(in_p, "xlo"), groups, expand, True, tile)
    dx_prev = shifted(in_o, "pipe", -1)

    grad_two = g2.astype(F32) + swapped(g2, "dp").astype(F32)
    grad_three = g3.astype(F32) + swapped(g3, "dp").astype(F32)
    grad_four = paired(g4o, g4p, 2, is_low)
    grad_one = paired(g1o, g1p, 3, is_low)
    return (
        y_next[None], dx_prev[None], grad_one[None], grad_two[None], grad_three[None], grad_four[None],
    )


def solution(mesh):
    parts = mesh.shape["tensor"]
    devices = mesh.devices.reshape(mesh.shape["dp"], mesh.shape["pipe"], 2, parts // 4, 2)
    fine = Mesh(devices, ("dp", "pipe", "xlo", "y", "core"))
    wide = ("xlo", "y", "core")
    acts = P("pipe", "dp", wide)
    five = P("pipe", wide, None, None, None)
    four = P("pipe", wide, None, None)
    return jax.shard_map(
        shards,
        mesh=fine,
        in_specs=(acts, acts, five, four, four, five),
        out_specs=(acts, acts, five, four, four, five),
        check_vma=False,
    )
```

```python
import functools
import math

import jax
import jax.numpy as jnp
from jax import lax
from jax.experimental import pallas as pl
from jax.experimental.pallas import tpu as pltpu
from jax.sharding import Mesh, PartitionSpec as P

BF = jnp.bfloat16
F32 = jnp.float32
GELU_A = math.sqrt(2.0 / math.pi)
GELU_B = 0.044715
YC = ("y", "core")
VMEM_MIB = 62
COST = 0.02


def params(mib):
    return pltpu.CompilerParams(vmem_limit_bytes=mib * 1024 * 1024)


def cost(flops, nbytes, trans=0):
    return pl.CostEstimate(flops=int(flops * COST), bytes_accessed=int(nbytes * COST), transcendentals=int(trans * COST))


def mm(a, b, dims):
    return lax.dot_general(a, b, (dims, ((), ())), preferred_element_type=F32)


def hot_key(shape, row_dim, sub):
    row = lax.broadcasted_iota(jnp.int32, shape, row_dim)
    col = lax.broadcasted_iota(jnp.int32, shape, 1 - row_dim)
    return jnp.where((row // sub) == (col // 2), row % sub - col % 2, -1)


def one_hot(key, group, k, sub):
    return jnp.where(key == group * (sub // 2) + k * 2, 1.0, 0.0).astype(BF)


def spread_weights(swap, f_ref, a_ref):
    groups, expand = f_ref.shape[0], f_ref.shape[1]
    rows, width = a_ref.shape
    wide = width // groups
    sub = groups * expand * 2
    key = hot_key((rows, 2 * rows // sub), 0, sub)
    for g in range(groups):
        pick = jnp.concatenate([one_hot(key, g, k, sub) for k in range(expand)], axis=1)
        if swap:
            source = jnp.concatenate([f_ref[g, k] for k in range(expand)], axis=1)
            value = mm(pick, source, ((1,), (1,)))
        else:
            value = mm(pick, f_ref[g].reshape(-1, wide), ((1,), (0,)))
        a_ref[:, g * wide : (g + 1) * wide] = value.astype(BF)


def lift_body(swaps, steps, side_ref, *refs):
    count = len(swaps)
    x_refs, f_refs, out_ref, a_refs = refs[:count], refs[count : 2 * count], refs[2 * count], refs[2 * count + 1 :]
    step = pl.program_id(0)
    for n in range(count):

        @pl.when(step == n * steps)
        def _(n=n):
            spread_weights(swaps[n], f_refs[n], a_refs[n])

        @pl.when((step >= n * steps) & (step < (n + 1) * steps))
        def _(n=n):
            value = mm(a_refs[n][...], x_refs[n][...], ((1,), (1,))).astype(BF)
            out_ref[...] = value.reshape(out_ref.shape)


def lift(xs, factors, swaps, side, peers, tile):
    count = len(xs)
    tokens, width = xs[0].shape
    steps = tokens // tile
    groups, expand = factors[0].shape[0], factors[0].shape[1]
    bsize = width // groups
    local = groups * expand
    rows = peers * local * local * 2
    cols = peers * local * 2
    x_specs, f_specs = [], []
    for n, swap in enumerate(swaps):
        x_specs.append(
            pl.BlockSpec((tile, width), lambda i, s, n=n: (jnp.clip(i - n * steps, 0, steps - 1), 0))
        )
        if swap:
            f_specs.append(pl.BlockSpec((groups, expand, bsize, cols), lambda i, s: (0, 0, 0, s[0])))
        else:
            f_specs.append(pl.BlockSpec((groups, expand, cols, bsize), lambda i, s: (0, 0, s[0], 0)))
    return pl.pallas_call(
        functools.partial(lift_body, swaps, steps),
        grid_spec=pltpu.PrefetchScalarGridSpec(
            num_scalar_prefetch=1,
            grid=(count * steps,),
            in_specs=x_specs + f_specs,
            out_specs=[
                pl.BlockSpec((peers, 1, rows // peers, tile), lambda i, s: (0, i // steps, 0, i % steps))
            ]
            + [pl.BlockSpec((rows, width), lambda i, s: (0, 0))] * count,
        ),
        out_shape=[jax.ShapeDtypeStruct((peers, count, rows // peers, tokens), BF)]
        + [jax.ShapeDtypeStruct((rows, width), BF)] * count,
        compiler_params=params(VMEM_MIB),
        cost_estimate=cost(4 * count * rows * width * tokens, 2 * count * tokens * (width + rows)),
        name="lift",
    )(side, *xs, *factors)


def gather_rows(scratch, side, own, peer):
    half = scratch.shape[0] // 2
    mine = pl.multiple_of(side * half, half)
    theirs = pl.multiple_of((1 - side) * half, half)
    scratch[pl.ds(mine, half), :] = own[...].reshape(half, scratch.shape[1])
    scratch[pl.ds(theirs, half), :] = peer[...].reshape(half, scratch.shape[1])


def split_rows(scratch, side, own, peer):
    half = scratch.shape[0] // 2
    mine = pl.multiple_of(side * half, half)
    theirs = pl.multiple_of((1 - side) * half, half)
    own[...] = scratch[pl.ds(mine, half), :].reshape(own.shape)
    peer[...] = scratch[pl.ds(theirs, half), :].reshape(peer.shape)


def forward_body(side_ref, ro_ref, rp_ref, w2_ref, w3_ref, out_ref, mixed, narrow):
    side = side_ref[0]
    gather_rows(mixed, side, ro_ref, rp_ref)
    pre = mm(w2_ref[0], mixed[...], ((0,), (0,)))
    act = (0.5 * pre * (1.0 + jnp.tanh(GELU_A * (pre + GELU_B * (pre * pre * pre))))).astype(BF)
    narrow[...] = mm(w3_ref[0], act, ((0,), (0,))).astype(BF)
    split_rows(narrow, side, out_ref.at[:, 0], out_ref.at[:, 1])


def plane_spec(array, plane, tile, start=0):
    peers, _, _, sub, _ = array.shape
    return pl.BlockSpec((peers, 1, 1, sub, tile), lambda c, i, s: (0, plane, start + c, 0, i))


def forward(side, own, peer, second, third, tile):
    peers, _, local, sub, tokens = own[0].shape
    bsize = second.shape[1]
    weight = pl.BlockSpec((1, bsize, bsize), lambda c, i, s: (c, 0, 0))
    return pl.pallas_call(
        forward_body,
        grid_spec=pltpu.PrefetchScalarGridSpec(
            num_scalar_prefetch=1,
            grid=(local, tokens // tile),
            in_specs=[plane_spec(*own, tile), plane_spec(*peer, tile), weight, weight],
            out_specs=pl.BlockSpec((peers, 2, 1, sub, tile), lambda c, i, s: (0, 0, c, 0, i)),
            scratch_shapes=[pltpu.VMEM((bsize, tile), BF), pltpu.VMEM((bsize, tile), BF)],
        ),
        out_shape=jax.ShapeDtypeStruct((peers, 2, local, sub, tokens), BF),
        compiler_params=params(VMEM_MIB),
        cost_estimate=cost(
            4 * local * bsize * bsize * tokens, 4 * local * bsize * tokens, local * bsize * tokens
        ),
        name="forward",
    )(side, own[0], peer[0], second, third)


def backward_body(
    steps, side_ref, ro_ref, rp_ref, go_ref, gp_ref, w2_ref, w3_ref, *rest,
):
    outs, (mixed, gnar, gmix, acc2, acc3) = rest[-8 - steps : -5], rest[-5:]
    mp_ref, g2_ref, g3_ref, mo_refs = outs[0], outs[1], outs[2], outs[3:]
    side = side_ref[0]
    step = pl.program_id(1)
    gather_rows(mixed, side, ro_ref, rp_ref)
    gather_rows(gnar, side, go_ref, gp_ref)
    pre = mm(w2_ref[0], mixed[...], ((0,), (0,)))
    square = pre * pre
    th = jnp.tanh(GELU_A * (pre + GELU_B * (square * pre)))
    half = 0.5 * (1.0 + th)
    act = (pre * half).astype(BF)
    slope = half + (0.5 * GELU_A) * pre * (1.0 - th * th) * (1.0 + (3.0 * GELU_B) * square)
    grad_act = mm(w3_ref[0], gnar[...], ((1,), (0,)))
    grad_pre = (grad_act * slope).astype(BF)
    gmix[...] = mm(w2_ref[0], grad_pre, ((1,), (0,))).astype(BF)
    for i, mo_ref in enumerate(mo_refs):

        @pl.when(step == i)
        def _(mo_ref=mo_ref):
            split_rows(gmix, side, mo_ref, mp_ref)

    add3 = mm(act, gnar[...], ((1,), (1,)))
    add2 = mm(mixed[...], grad_pre, ((1,), (1,)))

    @pl.when(step == 0)
    def _():
        acc2[...] = add2
        acc3[...] = add3

    @pl.when(step > 0)
    def _():
        acc2[...] += add2
        acc3[...] += add3

    @pl.when(step == pl.num_programs(1) - 1)
    def _():
        g2_ref[0] = acc2[...].astype(BF)
        g3_ref[0] = acc3[...].astype(BF)


def backward(side, own, peer, grad_own, grad_peer, second, third, tile, start, count, into):
    peers, _, local, sub, tokens = own[0].shape
    bsize = second.shape[1]
    steps = tokens // tile
    pieces = [plane_spec(*each, tile, start) for each in (own, peer, grad_own, grad_peer)]
    piece = pl.BlockSpec((peers, 1, sub, tile), lambda c, i, s: (0, start + c, 0, i))
    part = pl.BlockSpec((peers, 1, sub, tile), lambda c, i, s: (0, start + c, 0, 0))
    weight = pl.BlockSpec((1, bsize, bsize), lambda c, i, s: (start + c, 0, 0))
    grad = pl.BlockSpec((1, bsize, bsize), lambda c, i, s: (c, 0, 0))
    grads = jax.ShapeDtypeStruct((count, bsize, bsize), BF)
    extra = () if into is None else into
    return pl.pallas_call(
        functools.partial(backward_body, steps),
        grid_spec=pltpu.PrefetchScalarGridSpec(
            num_scalar_prefetch=1,
            grid=(count, tokens // tile),
            in_specs=pieces + [weight] * 2 + [pl.BlockSpec(memory_space=pl.ANY)] * len(extra),
            out_specs=[piece, grad, grad] + [part] * steps,
            scratch_shapes=[pltpu.VMEM((bsize, tile), BF)] * 3
            + [pltpu.VMEM((bsize, bsize), F32)] * 2,
        ),
        out_shape=[jax.ShapeDtypeStruct((peers, local, sub, tokens), BF), grads, grads]
        + [jax.ShapeDtypeStruct((peers, local, sub, tile), BF)] * steps,
        input_output_aliases={7 + i: (0 if i == 0 else 2 + i) for i in range(len(extra))},
        compiler_params=params(VMEM_MIB),
        cost_estimate=cost(
            10 * count * bsize * bsize * tokens, 6 * count * bsize * tokens, count * bsize * tokens
        ),
        name="backward",
    )(side, own[0], peer[0], grad_own[0], grad_peer[0], second, third, *extra)


def emit_body(add, s_ref, a_ref, *rest):
    prev_ref, out_ref = rest if add else (None, rest[0])
    value = mm(a_ref[...], s_ref[...].reshape(a_ref.shape[1], -1), ((1,), (0,))).T
    if add:
        value = value + prev_ref[...].astype(F32)
    out_ref[...] = value.astype(BF)


def emit(s, plane, a, prev, tile, start, tokens):
    width, rows = a.shape
    peers, _, each, _ = s.shape
    first = start // tile
    add = prev is not None
    wide = pl.BlockSpec((tile, width), lambda i: (i, 0))
    return pl.pallas_call(
        functools.partial(emit_body, add),
        grid=(tokens // tile,),
        in_specs=[
            pl.BlockSpec((peers, 1, each, tile), lambda i: (0, plane, 0, first + i)),
            pl.BlockSpec((width, rows), lambda i: (0, 0)),
        ]
        + ([wide] if add else []),
        out_specs=wide,
        out_shape=jax.ShapeDtypeStruct((tokens, width), BF),
        compiler_params=params(VMEM_MIB),
        cost_estimate=cost(2 * rows * width * tokens, 2 * tokens * (rows + 2 * width)),
        name="emit",
    )(*((s, a) + ((prev,) if add else ())))


def wgrad_body(swap, groups, expand, count, *refs):
    s_refs, (x_ref, g_ref, acc) = refs[:count], refs[count:]
    step = pl.program_id(0)
    rows, width = acc.shape
    wide = width // groups
    sub = groups * expand * 2
    cols = 2 * rows // sub

    for i in range(count):

        @pl.when(step == i)
        def _(i=i):
            more = mm(s_refs[i][...].reshape(rows, -1), x_ref[...], ((1,), (0,)))
            acc[...] = more if i == 0 else acc[...] + more

    @pl.when(step == count - 1)
    def _():
        key = hot_key((rows, cols) if swap else (cols, rows), 0 if swap else 1, sub)
        for g in range(groups):
            part = acc[:, g * wide : (g + 1) * wide].astype(BF)
            if swap:
                part = part.T
            picks = [one_hot(key, g, k, sub) for k in range(expand)]
            if swap:
                got = mm(part, jnp.concatenate(picks, axis=1), ((1,), (0,))).astype(BF)
            else:
                got = mm(jnp.concatenate(picks, axis=0), part, ((1,), (0,))).astype(BF)
            for k in range(expand):
                at = slice(k * cols, (k + 1) * cols)
                g_ref[g, k] = got[:, at] if swap else got[at]


def wgrad(s, x, groups, expand, swap):
    count = len(s)
    width = x.shape[1]
    tile = x.shape[0] // count
    peers, _, each, _ = s[0][0].shape
    rows = peers * each
    bsize = width // groups
    cols = rows // (groups * expand)
    grads = (groups, expand, bsize, cols) if swap else (groups, expand, cols, bsize)
    specs = [
        pl.BlockSpec((peers, 1, each, tile), lambda i, plane=plane, at=at: (0, plane, 0, at))
        for _, plane, at in s
    ]
    return pl.pallas_call(
        functools.partial(wgrad_body, swap, groups, expand, count),
        grid=(count,),
        in_specs=specs + [pl.BlockSpec((tile, width), lambda i: (i, 0))],
        out_specs=pl.BlockSpec(grads, lambda i: (0, 0, 0, 0)),
        scratch_shapes=[pltpu.VMEM((rows, width), F32)],
        out_shape=jax.ShapeDtypeStruct(grads, BF),
        compiler_params=params(VMEM_MIB),
        cost_estimate=cost(2 * rows * width * x.shape[0], 2 * x.shape[0] * (rows + width)),
        name="wgrad",
    )(*[array for array, _, _ in s], x)


def copied(value):
    return place(value, None, 0, 1)


def swapped(value, axes):
    count = lax.axis_size(axes)
    return lax.ppermute(value, axes, [(i, count - 1 - i) for i in range(count)])


def shifted(value, axis, steps):
    count = lax.axis_size(axis)
    leading, last = (max(0, -steps), min(count, count - steps))
    return lax.ppermute(value, axis, [(source, source + steps) for source in range(leading, last)])


def spread_out(value):
    return lax.all_to_all(value, YC, split_axis=0, concat_axis=0, tiled=True)


def behind(value, after):
    return value if after is None else lax.optimization_barrier((value, after))[0]


def halves(value, dim):
    size = value.shape[dim] // 2
    return lax.slice_in_dim(value, 0, size, axis=dim), lax.slice_in_dim(value, size, 2 * size, axis=dim)


def join_body(starts, sizes, *refs):
    out_ref = refs[-1]
    at = pl.program_id(0)
    for n, (start, size) in enumerate(zip(starts, sizes)):

        @pl.when((at >= start) & (at < start + size))
        def _(n=n):
            out_ref[...] = refs[2 * n][...].astype(F32) + refs[2 * n + 1][...].astype(F32)


def join(pairs):
    sizes = [a.shape[0] for a, _ in pairs]
    starts = [sum(sizes[:n]) for n in range(len(sizes))]
    rest = pairs[0][0].shape[1:]
    specs = []
    for start, size in zip(starts, sizes):
        spec = pl.BlockSpec(
            (1,) + rest, lambda i, start=start, size=size: (jnp.clip(i - start, 0, size - 1), 0, 0)
        )
        specs += [spec, spec]
    return pl.pallas_call(
        functools.partial(join_body, starts, sizes),
        grid=(sum(sizes),),
        in_specs=specs,
        out_specs=pl.BlockSpec((1,) + rest, lambda i: (i, 0, 0)),
        out_shape=jax.ShapeDtypeStruct((sum(sizes),) + rest, F32),
        compiler_params=params(VMEM_MIB),
        cost_estimate=cost(1, 1),
        name="join",
    )(*[each for pair in pairs for each in pair])


def paired_body(side_ref, ma_ref, mb_ref, ta_ref, tb_ref, out_ref):
    step = pl.program_id(0)

    @pl.when(step == 0)
    def _():
        out_ref[...] = ma_ref[...].astype(F32) + mb_ref[...].astype(F32)

    @pl.when(step == 1)
    def _():
        out_ref[...] = ta_ref[...].astype(F32) + tb_ref[...].astype(F32)


def paired(side, mine, theirs, dim):
    shape = mine[0].shape
    whole = pl.BlockSpec(shape, lambda i, s: (0,) * len(shape))

    def where(i, s):
        half = jnp.where(i == 0, s[0], 1 - s[0])
        return tuple(half if n == dim else 0 for n in range(len(shape)))

    full = tuple(2 * size if n == dim else size for n, size in enumerate(shape))
    return pl.pallas_call(
        paired_body,
        grid_spec=pltpu.PrefetchScalarGridSpec(
            num_scalar_prefetch=1,
            grid=(2,),
            in_specs=[whole] * 4,
            out_specs=pl.BlockSpec(shape, where),
        ),
        out_shape=jax.ShapeDtypeStruct(full, F32),
        compiler_params=params(VMEM_MIB),
        cost_estimate=cost(1, 1),
        name="paired",
    )(side, *mine, *theirs)


def place_body(value_ref, *rest):
    rest[-1][...] = value_ref[...]


def place(value, into, at, count):
    rows, width = value.shape
    extra = () if into is None else (into,)
    return pl.pallas_call(
        place_body,
        grid=(1,),
        in_specs=[pl.BlockSpec((rows, width), lambda i: (0, 0))]
        + [pl.BlockSpec(memory_space=pl.ANY)] * len(extra),
        out_specs=pl.BlockSpec((rows, width), lambda i: (at, 0)),
        out_shape=jax.ShapeDtypeStruct((count * rows, width), value.dtype),
        input_output_aliases={1: 0} if extra else {},
        compiler_params=params(VMEM_MIB),
        cost_estimate=cost(1, 1),
        name="place",
    )(value, *extra)


def shards(inputs, upstream, factor_one, factor_two, factor_three, factor_four):
    x, u = inputs[0], upstream[0]
    first, second, third, fourth = factor_one[0], factor_two[0], factor_three[0], factor_four[0]
    groups, expand, bsize = first.shape[0], first.shape[1], first.shape[2]
    local = groups * expand
    tokens = x.shape[0]
    peers = lax.axis_size("y") * lax.axis_size("core")
    low_or_high = lax.axis_index("xlo")
    is_low = low_or_high == 0
    side = low_or_high.astype(jnp.int32).reshape(1)
    zero = jnp.zeros((1,), jnp.int32)
    tile = 512 if tokens % 512 == 0 else tokens
    half = tokens // 2

    low, high = halves(first, 3)
    first_peer = swapped(jnp.where(is_low, high, low), "xlo")
    x_peer = swapped(x, "xlo")
    low, high = halves(fourth, 2)
    fourth_side = jnp.where(is_low, high, low)
    early = 2 * tokens // 3
    u_early = swapped(behind(u[:early], (x_peer, first_peer)), "xlo")
    u_late = swapped(behind(u[early:], u_early), "xlo")
    fourth_peer = swapped(behind(fourth_side, u_early), "xlo")
    u_peer = jnp.concatenate([u_early, u_late], axis=0)

    def inner(value, after=None):
        return spread_out(behind(value, after)).reshape(peers, -1, local, 2 * local, tokens)

    def outer(value, after):
        value = value.reshape(peers, -1, 2 * local * local, value.shape[-1])
        return spread_out(behind(value, after))

    l12, a1o, a4o = lift([x, u], [first, fourth], [True, False], side, peers, tile)
    y12 = inner(l12)
    l1p, a1p = lift([x_peer], [first_peer], [True], zero, peers, tile)
    y1p = inner(l1p, (y12, u_early))
    l2p, a4p = lift([u_peer], [fourth_peer], [False], zero, peers, tile)
    y2p = inner(l2p, y1p)
    a1o, a4o, a1p, a4p = a1o.T, a4o.T, a1p.T, a4p.T
    n = forward(behind(side, (a1o, a4o, a1p, a4p)), (y12, 0), (y1p, 0), second, third, half)
    y3 = outer(n, y2p)

    args = ((y12, 0), (y1p, 0), (y12, 1), (y2p, 0), second, third, half)
    third_part = -(-local // 3)
    cuts = [0, third_part, 2 * third_part, local]
    into, g2, g3, d2, d3 = None, [], [], [], []
    gate = side
    for n in range(3):
        got = backward(gate, *args, cuts[n], cuts[n + 1] - cuts[n], into)
        mp, mo1, mo2 = into = (got[0], got[3], got[4])
        g2.append(got[1])
        g3.append(got[2])
        d2.append(swapped(got[1], "dp"))
        d3.append(swapped(got[2], "dp"))
        if n == 1:
            gate = behind(side, (d2[0], d3[0]))
    y4p = outer(mp, (y3, *d2, *d3))
    out_p = emit(y3, 1, a4p, None, half, 0, tokens)
    out_peer = swapped(out_p, "xlo")
    g4p = wgrad([(y3, 1, 0), (y3, 1, 1)], behind(u_peer, out_p), groups, expand, False)
    g4o = wgrad([(y3, 0, 0), (y3, 0, 1)], u, groups, expand, False)
    grad_two = join(list(zip(g2, d2)))
    grad_three = join(list(zip(g3, d3)))
    y4a = outer(mo1, (y4p, g4o, g4p, grad_two, grad_three))
    t4x = swapped(behind(g4p, out_peer), "xlo")
    t4d = swapped(behind(g4p, out_peer), ("dp", "xlo"))
    out_o = emit(y3, 0, a4o, out_peer, half, 0, tokens)
    y_next = copied(shifted(out_o, "pipe", 1))
    in_p1 = emit(y4p, 0, a1p, None, half, 0, half)
    in_p2 = emit(y4p, 0, a1p, None, half, half, half)
    in_peer1 = swapped(behind(in_p1, (t4x, t4d, out_o)), "xlo")
    in_peer2 = swapped(behind(in_p2, in_peer1), "xlo")
    g1p = wgrad([(y4p, 0, 0), (y4p, 0, 1)], behind(x_peer, in_p2), groups, expand, True)
    y4b = outer(mo2, (y4a, in_p2))
    d4o = swapped(behind(g4o, in_peer2), "dp")
    in_a = emit(y4a, 0, a1o, in_peer1, half, 0, half)
    dx1 = shifted(in_a, "pipe", -1)
    t1x = swapped(behind(g1p, in_peer2), "xlo")
    t1d = swapped(behind(g1p, in_peer2), ("dp", "xlo"))
    in_b = emit(y4b, 0, a1o, behind(in_peer2, g1p), half, 0, half)
    dx2 = shifted(in_b, "pipe", -1)
    dx_prev = place(dx1, None, 0, 2)
    g1o = wgrad(
        [(y4a, 0, 0), (y4b, 0, 0)],
        behind(x, in_b),
        groups, expand, True,
    )
    d1o = behind(swapped(g1o, "dp"), dx2)
    grad_four = paired(side, (g4o, d4o), (t4x, t4d), 2)
    grad_one = paired(side, (g1o, d1o), (t1x, t1d), 3)
    dx_prev = place(dx2, dx_prev, 1, 2)
    return (
        y_next[None], dx_prev[None], grad_one[None], grad_two[None], grad_three[None], grad_four[None],
    )


def solution(mesh):
    parts = mesh.shape["tensor"]
    devices = mesh.devices.reshape(mesh.shape["dp"], mesh.shape["pipe"], 2, parts // 4, 2)
    fine = Mesh(devices, ("dp", "pipe", "xlo", "y", "core"))
    wide = ("xlo", "y", "core")
    acts = P("pipe", "dp", wide)
    five = P("pipe", wide, None, None, None)
    four = P("pipe", wide, None, None)
    return jax.shard_map(
        shards,
        mesh=fine,
        in_specs=(acts, acts, five, four, four, five),
        out_specs=(acts, acts, five, four, four, five),
        check_vma=False,
    )
```

```python
import functools
import math

import jax
import jax.numpy as jnp
from jax import lax
from jax.experimental import pallas as pl
from jax.experimental.pallas import tpu as pltpu
from jax.sharding import Mesh, PartitionSpec as P

BF = jnp.bfloat16
F32 = jnp.float32
GELU_A = math.sqrt(2.0 / math.pi)
GELU_B = 0.044715
YC = ("y", "core")
VMEM_MIB = 62
COST = 0.02


def params(mib):
    return pltpu.CompilerParams(vmem_limit_bytes=mib * 1024 * 1024)


def cost(flops, nbytes, trans=0):
    return pl.CostEstimate(flops=int(flops * COST), bytes_accessed=int(nbytes * COST), transcendentals=int(trans * COST))


def mm(a, b, dims):
    return lax.dot_general(a, b, (dims, ((), ())), preferred_element_type=F32)


def hot_key(shape, row_dim, sub):
    row = lax.broadcasted_iota(jnp.int32, shape, row_dim)
    col = lax.broadcasted_iota(jnp.int32, shape, 1 - row_dim)
    return jnp.where((row // sub) == (col // 2), row % sub - col % 2, -1)


def one_hot(key, group, k, sub):
    return jnp.where(key == group * (sub // 2) + k * 2, 1.0, 0.0).astype(BF)


def spread_weights(swap, f_ref, a_ref):
    groups, expand = f_ref.shape[0], f_ref.shape[1]
    rows, width = a_ref.shape
    wide = width // groups
    sub = groups * expand * 2
    key = hot_key((rows, 2 * rows // sub), 0, sub)
    for g in range(groups):
        pick = jnp.concatenate([one_hot(key, g, k, sub) for k in range(expand)], axis=1)
        if swap:
            source = jnp.concatenate([f_ref[g, k] for k in range(expand)], axis=1)
            value = mm(pick, source, ((1,), (1,)))
        else:
            value = mm(pick, f_ref[g].reshape(-1, wide), ((1,), (0,)))
        a_ref[:, g * wide : (g + 1) * wide] = value.astype(BF)


def lift_body(swaps, steps, side_ref, *refs):
    count = len(swaps)
    x_refs, f_refs, out_ref, a_refs = refs[:count], refs[count : 2 * count], refs[2 * count], refs[2 * count + 1 :]
    step = pl.program_id(0)
    for n in range(count):

        @pl.when(step == n * steps)
        def _(n=n):
            spread_weights(swaps[n], f_refs[n], a_refs[n])

        @pl.when((step >= n * steps) & (step < (n + 1) * steps))
        def _(n=n):
            value = mm(a_refs[n][...], x_refs[n][...], ((1,), (1,))).astype(BF)
            out_ref[...] = value.reshape(out_ref.shape)


def lift(xs, factors, swaps, side, peers, tile):
    count = len(xs)
    tokens, width = xs[0].shape
    steps = tokens // tile
    groups, expand = factors[0].shape[0], factors[0].shape[1]
    bsize = width // groups
    local = groups * expand
    rows = peers * local * local * 2
    cols = peers * local * 2
    x_specs, f_specs = [], []
    for n, swap in enumerate(swaps):
        x_specs.append(
            pl.BlockSpec((tile, width), lambda i, s, n=n: (jnp.clip(i - n * steps, 0, steps - 1), 0))
        )
        if swap:
            f_specs.append(pl.BlockSpec((groups, expand, bsize, cols), lambda i, s: (0, 0, 0, s[0])))
        else:
            f_specs.append(pl.BlockSpec((groups, expand, cols, bsize), lambda i, s: (0, 0, s[0], 0)))
    return pl.pallas_call(
        functools.partial(lift_body, swaps, steps),
        grid_spec=pltpu.PrefetchScalarGridSpec(
            num_scalar_prefetch=1,
            grid=(count * steps,),
            in_specs=x_specs + f_specs,
            out_specs=[
                pl.BlockSpec((peers, 1, rows // peers, tile), lambda i, s: (0, i // steps, 0, i % steps))
            ]
            + [pl.BlockSpec((rows, width), lambda i, s: (0, 0))] * count,
        ),
        out_shape=[jax.ShapeDtypeStruct((peers, count, rows // peers, tokens), BF)]
        + [jax.ShapeDtypeStruct((rows, width), BF)] * count,
        compiler_params=params(VMEM_MIB),
        cost_estimate=cost(4 * count * rows * width * tokens, 2 * count * tokens * (width + rows)),
        name="lift",
    )(side, *xs, *factors)


def gather_rows(scratch, side, own, peer):
    half = scratch.shape[0] // 2
    mine = pl.multiple_of(side * half, half)
    theirs = pl.multiple_of((1 - side) * half, half)
    scratch[pl.ds(mine, half), :] = own[...].reshape(half, scratch.shape[1])
    scratch[pl.ds(theirs, half), :] = peer[...].reshape(half, scratch.shape[1])


def split_rows(scratch, side, own, peer):
    half = scratch.shape[0] // 2
    mine = pl.multiple_of(side * half, half)
    theirs = pl.multiple_of((1 - side) * half, half)
    own[...] = scratch[pl.ds(mine, half), :].reshape(own.shape)
    peer[...] = scratch[pl.ds(theirs, half), :].reshape(peer.shape)


def forward_body(side_ref, ro_ref, rp_ref, w2_ref, w3_ref, own_ref, peer_ref, mixed, narrow):
    side = side_ref[0]
    gather_rows(mixed, side, ro_ref, rp_ref)
    pre = mm(w2_ref[0], mixed[...], ((0,), (0,)))
    act = (0.5 * pre * (1.0 + jnp.tanh(GELU_A * (pre + GELU_B * (pre * pre * pre))))).astype(BF)
    narrow[...] = mm(w3_ref[0], act, ((0,), (0,))).astype(BF)
    split_rows(narrow, side, own_ref, peer_ref)


def plane_spec(array, plane, tile, start=0):
    peers, _, _, sub, _ = array.shape
    return pl.BlockSpec((peers, 1, 1, sub, tile), lambda c, i, s: (0, plane, start + c, 0, i))


def forward(side, own, peer, second, third, tile):
    peers, _, local, sub, tokens = own[0].shape
    bsize = second.shape[1]
    weight = pl.BlockSpec((1, bsize, bsize), lambda c, i, s: (c, 0, 0))
    return pl.pallas_call(
        forward_body,
        grid_spec=pltpu.PrefetchScalarGridSpec(
            num_scalar_prefetch=1,
            grid=(local, tokens // tile),
            in_specs=[plane_spec(*own, tile), plane_spec(*peer, tile), weight, weight],
            out_specs=[pl.BlockSpec((peers, 1, sub, tile), lambda c, i, s: (0, c, 0, i))] * 2,
            scratch_shapes=[pltpu.VMEM((bsize, tile), BF), pltpu.VMEM((bsize, tile), BF)],
        ),
        out_shape=[jax.ShapeDtypeStruct((peers, local, sub, tokens), BF)] * 2,
        compiler_params=params(VMEM_MIB),
        cost_estimate=cost(
            4 * local * bsize * bsize * tokens, 4 * local * bsize * tokens, local * bsize * tokens
        ),
        name="forward",
    )(side, own[0], peer[0], second, third)


def backward_body(
    steps, side_ref, ro_ref, rp_ref, go_ref, gp_ref, w2_ref, w3_ref, *rest,
):
    outs, (mixed, gnar, gmix, acc2, acc3) = rest[-7 - steps : -5], rest[-5:]
    mp_ref, g_ref, mo_refs = outs[0], outs[1], outs[2:]
    side = side_ref[0]
    step = pl.program_id(1)
    gather_rows(mixed, side, ro_ref, rp_ref)
    gather_rows(gnar, side, go_ref, gp_ref)
    pre = mm(w2_ref[0], mixed[...], ((0,), (0,)))
    square = pre * pre
    th = jnp.tanh(GELU_A * (pre + GELU_B * (square * pre)))
    half = 0.5 * (1.0 + th)
    act = (pre * half).astype(BF)
    slope = half + (0.5 * GELU_A) * pre * (1.0 - th * th) * (1.0 + (3.0 * GELU_B) * square)
    grad_act = mm(w3_ref[0], gnar[...], ((1,), (0,)))
    grad_pre = (grad_act * slope).astype(BF)
    gmix[...] = mm(w2_ref[0], grad_pre, ((1,), (0,))).astype(BF)
    for i, mo_ref in enumerate(mo_refs):

        @pl.when(step == i)
        def _(mo_ref=mo_ref):
            split_rows(gmix, side, mo_ref, mp_ref)

    add3 = mm(act, gnar[...], ((1,), (1,)))
    add2 = mm(mixed[...], grad_pre, ((1,), (1,)))

    @pl.when(step == 0)
    def _():
        acc2[...] = add2
        acc3[...] = add3

    @pl.when(step > 0)
    def _():
        acc2[...] += add2
        acc3[...] += add3

    @pl.when(step == pl.num_programs(1) - 1)
    def _():
        g_ref[0, 0] = acc2[...].astype(BF)
        g_ref[1, 0] = acc3[...].astype(BF)


def backward(side, own, peer, grad_own, grad_peer, second, third, tile, start, count, into):
    peers, _, local, sub, tokens = own[0].shape
    bsize = second.shape[1]
    steps = tokens // tile
    pieces = [plane_spec(*each, tile, start) for each in (own, peer, grad_own, grad_peer)]
    piece = pl.BlockSpec((peers, 1, sub, tile), lambda c, i, s: (0, start + c, 0, i))
    part = pl.BlockSpec((peers, 1, sub, tile), lambda c, i, s: (0, start + c, 0, 0))
    weight = pl.BlockSpec((1, bsize, bsize), lambda c, i, s: (start + c, 0, 0))
    grad = pl.BlockSpec((2, 1, bsize, bsize), lambda c, i, s: (0, c, 0, 0))
    grads = jax.ShapeDtypeStruct((2, count, bsize, bsize), BF)
    extra = () if into is None else into
    return pl.pallas_call(
        functools.partial(backward_body, steps),
        grid_spec=pltpu.PrefetchScalarGridSpec(
            num_scalar_prefetch=1,
            grid=(count, tokens // tile),
            in_specs=pieces + [weight] * 2 + [pl.BlockSpec(memory_space=pl.ANY)] * len(extra),
            out_specs=[piece, grad] + [part] * steps,
            scratch_shapes=[pltpu.VMEM((bsize, tile), BF)] * 3
            + [pltpu.VMEM((bsize, bsize), F32)] * 2,
        ),
        out_shape=[jax.ShapeDtypeStruct((peers, local, sub, tokens), BF), grads]
        + [jax.ShapeDtypeStruct((peers, local, sub, tile), BF)] * steps,
        input_output_aliases={7 + i: (0 if i == 0 else 1 + i) for i in range(len(extra))},
        compiler_params=params(VMEM_MIB),
        cost_estimate=cost(
            10 * count * bsize * bsize * tokens, 6 * count * bsize * tokens, count * bsize * tokens
        ),
        name="backward",
    )(side, own[0], peer[0], grad_own[0], grad_peer[0], second, third, *extra)


def emit_body(add, s_ref, a_ref, *rest):
    prev_ref, out_ref = rest if add else (None, rest[0])
    value = mm(a_ref[...], s_ref[...].reshape(a_ref.shape[1], -1), ((1,), (0,))).T
    if add:
        value = value + prev_ref[...].astype(F32)
    out_ref[...] = value.astype(BF)


def emit(s, plane, a, prev, tile, start, tokens):
    width, rows = a.shape
    peers, _, each, _ = s.shape
    first = start // tile
    add = prev is not None
    wide = pl.BlockSpec((tile, width), lambda i: (i, 0))
    return pl.pallas_call(
        functools.partial(emit_body, add),
        grid=(tokens // tile,),
        in_specs=[
            pl.BlockSpec((peers, 1, each, tile), lambda i: (0, plane, 0, first + i)),
            pl.BlockSpec((width, rows), lambda i: (0, 0)),
        ]
        + ([wide] if add else []),
        out_specs=wide,
        out_shape=jax.ShapeDtypeStruct((tokens, width), BF),
        compiler_params=params(VMEM_MIB),
        cost_estimate=cost(2 * rows * width * tokens, 2 * tokens * (rows + 2 * width)),
        name="emit",
    )(*((s, a) + ((prev,) if add else ())))


def wgrad_body(swap, groups, expand, count, *refs):
    s_refs, (x_ref, g_ref, acc) = refs[:count], refs[count:]
    step = pl.program_id(0)
    rows, width = acc.shape
    wide = width // groups
    sub = groups * expand * 2
    cols = 2 * rows // sub

    for i in range(count):

        @pl.when(step == i)
        def _(i=i):
            more = mm(s_refs[i][...].reshape(rows, -1), x_ref[...], ((1,), (0,)))
            acc[...] = more if i == 0 else acc[...] + more

    @pl.when(step == count - 1)
    def _():
        key = hot_key((rows, cols) if swap else (cols, rows), 0 if swap else 1, sub)
        for g in range(groups):
            part = acc[:, g * wide : (g + 1) * wide].astype(BF)
            if swap:
                part = part.T
            picks = [one_hot(key, g, k, sub) for k in range(expand)]
            if swap:
                got = mm(part, jnp.concatenate(picks, axis=1), ((1,), (0,))).astype(BF)
            else:
                got = mm(jnp.concatenate(picks, axis=0), part, ((1,), (0,))).astype(BF)
            for k in range(expand):
                at = slice(k * cols, (k + 1) * cols)
                g_ref[g, k] = got[:, at] if swap else got[at]


def wgrad(s, x, groups, expand, swap):
    count = len(s)
    width = x.shape[1]
    tile = x.shape[0] // count
    peers, _, each, _ = s[0][0].shape
    rows = peers * each
    bsize = width // groups
    cols = rows // (groups * expand)
    grads = (groups, expand, bsize, cols) if swap else (groups, expand, cols, bsize)
    specs = [
        pl.BlockSpec((peers, 1, each, tile), lambda i, plane=plane, at=at: (0, plane, 0, at))
        for _, plane, at in s
    ]
    return pl.pallas_call(
        functools.partial(wgrad_body, swap, groups, expand, count),
        grid=(count,),
        in_specs=specs + [pl.BlockSpec((tile, width), lambda i: (i, 0))],
        out_specs=pl.BlockSpec(grads, lambda i: (0, 0, 0, 0)),
        scratch_shapes=[pltpu.VMEM((rows, width), F32)],
        out_shape=jax.ShapeDtypeStruct(grads, BF),
        compiler_params=params(VMEM_MIB),
        cost_estimate=cost(2 * rows * width * x.shape[0], 2 * x.shape[0] * (rows + width)),
        name="wgrad",
    )(*[array for array, _, _ in s], x)


def copied(value):
    return place(value, None, 0, 1)


def swapped(value, axes):
    count = lax.axis_size(axes)
    return lax.ppermute(value, axes, [(i, count - 1 - i) for i in range(count)])


def shifted(value, axis, steps):
    count = lax.axis_size(axis)
    leading, last = (max(0, -steps), min(count, count - steps))
    return lax.ppermute(value, axis, [(source, source + steps) for source in range(leading, last)])


def spread_out(value):
    return lax.all_to_all(value, YC, split_axis=0, concat_axis=0, tiled=True)


def behind(value, after):
    return value if after is None else lax.optimization_barrier((value, after))[0]


def halves(value, dim):
    size = value.shape[dim] // 2
    return lax.slice_in_dim(value, 0, size, axis=dim), lax.slice_in_dim(value, size, 2 * size, axis=dim)


def join_body(count, *refs):
    out_refs = refs[2 * count :]
    start = 0
    for n in range(count):
        size = refs[2 * n].shape[1]
        for which, out_ref in enumerate(out_refs):
            out_ref[start : start + size] = refs[2 * n][which].astype(F32) + refs[2 * n + 1][which].astype(F32)
        start += size


def join(pairs):
    arrays = [each for pair in pairs for each in pair]
    results = arrays[0].shape[0]
    rest = arrays[0].shape[2:]
    total = (sum(a.shape[1] for a, _ in pairs),) + rest
    return pl.pallas_call(
        functools.partial(join_body, len(pairs)),
        grid=(1,),
        in_specs=[pl.BlockSpec(each.shape, lambda i: (0, 0, 0, 0)) for each in arrays],
        out_specs=[pl.BlockSpec(total, lambda i: (0, 0, 0))] * results,
        out_shape=[jax.ShapeDtypeStruct(total, F32)] * results,
        compiler_params=params(VMEM_MIB),
        cost_estimate=cost(1, 1),
        name="join",
    )(*arrays)


def paired_body(side_ref, ma_ref, mb_ref, ta_ref, tb_ref, out_ref):
    step = pl.program_id(0)

    @pl.when(step == 0)
    def _():
        out_ref[...] = ma_ref[...].astype(F32) + mb_ref[...].astype(F32)

    @pl.when(step == 1)
    def _():
        out_ref[...] = ta_ref[...].astype(F32) + tb_ref[...].astype(F32)


def paired(side, mine, theirs, dim):
    shape = mine[0].shape
    whole = pl.BlockSpec(shape, lambda i, s: (0,) * len(shape))

    def where(i, s):
        half = jnp.where(i == 0, s[0], 1 - s[0])
        return tuple(half if n == dim else 0 for n in range(len(shape)))

    full = tuple(2 * size if n == dim else size for n, size in enumerate(shape))
    return pl.pallas_call(
        paired_body,
        grid_spec=pltpu.PrefetchScalarGridSpec(
            num_scalar_prefetch=1,
            grid=(2,),
            in_specs=[whole] * 4,
            out_specs=pl.BlockSpec(shape, where),
        ),
        out_shape=jax.ShapeDtypeStruct(full, F32),
        compiler_params=params(VMEM_MIB),
        cost_estimate=cost(1, 1),
        name="paired",
    )(side, *mine, *theirs)


def place_body(value_ref, *rest):
    rest[-1][...] = value_ref[...]


def place(value, into, at, count):
    rows, width = value.shape
    extra = () if into is None else (into,)
    return pl.pallas_call(
        place_body,
        grid=(1,),
        in_specs=[pl.BlockSpec((rows, width), lambda i: (0, 0))]
        + [pl.BlockSpec(memory_space=pl.ANY)] * len(extra),
        out_specs=pl.BlockSpec((rows, width), lambda i: (at, 0)),
        out_shape=jax.ShapeDtypeStruct((count * rows, width), value.dtype),
        input_output_aliases={1: 0} if extra else {},
        compiler_params=params(VMEM_MIB),
        cost_estimate=cost(1, 1),
        name="place",
    )(value, *extra)


def shards(inputs, upstream, factor_one, factor_two, factor_three, factor_four):
    x, u = inputs[0], upstream[0]
    first, second, third, fourth = factor_one[0], factor_two[0], factor_three[0], factor_four[0]
    groups, expand, bsize = first.shape[0], first.shape[1], first.shape[2]
    local = groups * expand
    tokens = x.shape[0]
    peers = lax.axis_size("y") * lax.axis_size("core")
    low_or_high = lax.axis_index("xlo")
    is_low = low_or_high == 0
    side = low_or_high.astype(jnp.int32).reshape(1)
    zero = jnp.zeros((1,), jnp.int32)
    half = tokens // 2
    tile = half

    low, high = halves(first, 3)
    first_peer = swapped(jnp.where(is_low, high, low), "xlo")
    x_peer = swapped(x, "xlo")
    low, high = halves(fourth, 2)
    fourth_side = jnp.where(is_low, high, low)
    early = half
    u_early = swapped(behind(u[:early], (x_peer, first_peer)), "xlo")
    u_late = swapped(behind(u[early:], u_early), "xlo")
    fourth_peer = swapped(behind(fourth_side, u_early), "xlo")
    u_peer = jnp.concatenate([u_early, u_late], axis=0)

    def inner(value, after=None):
        return spread_out(behind(value, after)).reshape(peers, -1, local, 2 * local, tokens)

    def outer(value, after):
        value = value.reshape(peers, -1, 2 * local * local, value.shape[-1])
        return spread_out(behind(value, after))

    l12, a1o, a4o = lift([x, u], [first, fourth], [True, False], side, peers, tile)
    y12 = inner(l12)
    l1p, a1p = lift([x_peer], [first_peer], [True], zero, peers, tile)
    y1p = inner(l1p, (y12, u_early))
    l2p, a4p = lift([u_peer], [fourth_peer], [False], zero, peers, tile)
    y2p = inner(l2p, y1p)
    a1o, a4o, a1p, a4p = a1o.T, a4o.T, a1p.T, a4p.T
    no, np_ = forward(behind(side, (a1o, a4o, a1p, a4p)), (y12, 0), (y1p, 0), second, third, half)
    y3p = outer(np_, y2p)
    args = ((y12, 0), (y1p, 0), (y12, 1), (y2p, 0), second, third, half)
    first_cut, second_cut = 3 * local // 8, local // 2
    mp, ga, mo1, mo2 = backward(side, *args, 0, first_cut, None)
    da = swapped(ga, "dp")
    mp, gb, mo1, mo2 = backward(side, *args, first_cut, second_cut - first_cut, (mp, mo1, mo2))
    mp, gc, mo1, mo2 = backward(side, *args, second_cut, local - second_cut, (mp, mo1, mo2))
    y3o = outer(no, (y3p, mp, da))
    out_p = emit(y3p, 0, a4p, None, half, 0, tokens)
    out_peer = swapped(out_p, "xlo")
    g4p = wgrad([(y3p, 0, 0), (y3p, 0, 1)], behind(u_peer, out_p), groups, expand, False)
    y4p = outer(mp, (y3o, g4p, out_peer))
    db = swapped(behind(gb, out_peer), "dp")
    dc = swapped(behind(gc, out_peer), "dp")
    t4x, t4d = swapped(behind(g4p, out_peer), "xlo"), swapped(behind(g4p, out_peer), ("dp", "xlo"))
    out_o = emit(y3o, 0, a4o, out_peer, half, 0, tokens)
    y_next = copied(shifted(out_o, "pipe", 1))
    g4o = wgrad([(y3o, 0, 0), (y3o, 0, 1)], behind(u, out_o), groups, expand, False)
    y4a = outer(mo1, (y4p, g4o, db, dc, t4x, t4d))
    grad_two, grad_three = join([(ga, da), (gb, db), (gc, dc)])
    in_p1 = emit(y4p, 0, a1p, None, half, 0, half)
    in_peer1 = swapped(behind(in_p1, out_peer), "xlo")
    in_p2 = emit(y4p, 0, a1p, None, half, half, half)
    in_peer2 = swapped(in_p2, "xlo")
    g1p = wgrad([(y4p, 0, 0), (y4p, 0, 1)], behind(x_peer, in_p2), groups, expand, True)
    d4o = swapped(g4o, "dp")
    y4b = outer(mo2, (y4a, g1p, y_next, d4o))
    in_a = emit(y4a, 0, a1o, behind(in_peer1, g1p), half, 0, half)
    dx1 = shifted(in_a, "pipe", -1)
    late = (in_peer2, in_a, grad_two, grad_three)
    t1x, t1d = swapped(behind(g1p, late), "xlo"), swapped(behind(g1p, late), ("dp", "xlo"))
    in_b = emit(y4b, 0, a1o, in_peer2, half, 0, half)
    dx2 = shifted(behind(in_b, dx1), "pipe", -1)
    dx_prev = place(dx1, None, 0, 2)
    g1o = wgrad(
        [(y4a, 0, 0), (y4b, 0, 0)],
        behind(x, in_b),
        groups, expand, True,
    )
    d1o = swapped(behind(g1o, (t1x, t1d)), "dp")
    grad_four = paired(side, (g4o, d4o), (t4x, t4d), 2)
    dx_prev = place(dx2, dx_prev, 1, 2)
    grad_one = paired(side, (behind(g1o, (dx_prev, grad_four)), d1o), (t1x, t1d), 3)
    return (
        y_next[None], dx_prev[None], grad_one[None], grad_two[None], grad_three[None], grad_four[None],
    )


def solution(mesh):
    parts = mesh.shape["tensor"]
    devices = mesh.devices.reshape(mesh.shape["dp"], mesh.shape["pipe"], 2, parts // 4, 2)
    fine = Mesh(devices, ("dp", "pipe", "xlo", "y", "core"))
    wide = ("xlo", "y", "core")
    acts = P("pipe", "dp", wide)
    five = P("pipe", wide, None, None, None)
    four = P("pipe", wide, None, None)
    return jax.shard_map(
        shards,
        mesh=fine,
        in_specs=(acts, acts, five, four, four, five),
        out_specs=(acts, acts, five, four, four, five),
        check_vma=False,
    )
```

```python
import functools
import math

import jax
import jax.numpy as jnp
from jax import lax
from jax.experimental import pallas as pl
from jax.experimental.pallas import tpu as pltpu
from jax.sharding import Mesh, PartitionSpec as P

BF = jnp.bfloat16
F32 = jnp.float32
GELU_A = math.sqrt(2.0 / math.pi)
GELU_B = 0.044715
YC = ("y", "core")
VMEM_MIB = 62
COST = 0.02


def params(mib):
    return pltpu.CompilerParams(vmem_limit_bytes=mib * 1024 * 1024)


def cost(flops, nbytes, trans=0):
    return pl.CostEstimate(flops=int(flops * COST), bytes_accessed=int(nbytes * COST), transcendentals=int(trans * COST))


def mm(a, b, dims):
    return lax.dot_general(a, b, (dims, ((), ())), preferred_element_type=F32)


def hot_key(shape, row_dim, sub):
    row = lax.broadcasted_iota(jnp.int32, shape, row_dim)
    col = lax.broadcasted_iota(jnp.int32, shape, 1 - row_dim)
    return jnp.where((row // sub) == (col // 2), row % sub - col % 2, -1)


def one_hot(key, group, k, sub):
    return jnp.where(key == group * (sub // 2) + k * 2, 1.0, 0.0).astype(BF)


def spread_weights(swap, f_ref, a_ref):
    groups, expand = f_ref.shape[0], f_ref.shape[1]
    rows, width = a_ref.shape
    wide = width // groups
    sub = groups * expand * 2
    key = hot_key((rows, 2 * rows // sub), 0, sub)
    for g in range(groups):
        pick = jnp.concatenate([one_hot(key, g, k, sub) for k in range(expand)], axis=1)
        if swap:
            source = jnp.concatenate([f_ref[g, k] for k in range(expand)], axis=1)
            value = mm(pick, source, ((1,), (1,)))
        else:
            value = mm(pick, f_ref[g].reshape(-1, wide), ((1,), (0,)))
        a_ref[:, g * wide : (g + 1) * wide] = value.astype(BF)


def lift_body(swaps, steps, side_ref, *refs):
    count = len(swaps)
    x_refs, f_refs, out_ref, a_refs = refs[:count], refs[count : 2 * count], refs[2 * count], refs[2 * count + 1 :]
    step = pl.program_id(0)
    for n in range(count):

        @pl.when(step == n * steps)
        def _(n=n):
            spread_weights(swaps[n], f_refs[n], a_refs[n])

        @pl.when((step >= n * steps) & (step < (n + 1) * steps))
        def _(n=n):
            value = mm(a_refs[n][...], x_refs[n][...], ((1,), (1,))).astype(BF)
            out_ref[...] = value.reshape(out_ref.shape)


def lift(xs, factors, swaps, side, peers, tile):
    count = len(xs)
    tokens, width = xs[0].shape
    steps = tokens // tile
    groups, expand = factors[0].shape[0], factors[0].shape[1]
    bsize = width // groups
    local = groups * expand
    rows = peers * local * local * 2
    cols = peers * local * 2
    x_specs, f_specs = [], []
    for n, swap in enumerate(swaps):
        x_specs.append(
            pl.BlockSpec((tile, width), lambda i, s, n=n: (jnp.clip(i - n * steps, 0, steps - 1), 0))
        )
        if swap:
            f_specs.append(pl.BlockSpec((groups, expand, bsize, cols), lambda i, s: (0, 0, 0, s[0])))
        else:
            f_specs.append(pl.BlockSpec((groups, expand, cols, bsize), lambda i, s: (0, 0, s[0], 0)))
    return pl.pallas_call(
        functools.partial(lift_body, swaps, steps),
        grid_spec=pltpu.PrefetchScalarGridSpec(
            num_scalar_prefetch=1,
            grid=(count * steps,),
            in_specs=x_specs + f_specs,
            out_specs=[
                pl.BlockSpec((peers, 1, rows // peers, tile), lambda i, s: (0, i // steps, 0, i % steps))
            ]
            + [pl.BlockSpec((rows, width), lambda i, s: (0, 0))] * count,
        ),
        out_shape=[jax.ShapeDtypeStruct((peers, count, rows // peers, tokens), BF)]
        + [jax.ShapeDtypeStruct((rows, width), BF)] * count,
        compiler_params=params(VMEM_MIB),
        cost_estimate=cost(4 * count * rows * width * tokens, 2 * count * tokens * (width + rows)),
        name="lift",
    )(side, *xs, *factors)


def gather_rows(scratch, side, own, peer):
    half = scratch.shape[0] // 2
    mine = pl.multiple_of(side * half, half)
    theirs = pl.multiple_of((1 - side) * half, half)
    scratch[pl.ds(mine, half), :] = own[...].reshape(half, scratch.shape[1])
    scratch[pl.ds(theirs, half), :] = peer[...].reshape(half, scratch.shape[1])


def split_rows(scratch, side, own, peer):
    half = scratch.shape[0] // 2
    mine = pl.multiple_of(side * half, half)
    theirs = pl.multiple_of((1 - side) * half, half)
    own[...] = scratch[pl.ds(mine, half), :].reshape(own.shape)
    peer[...] = scratch[pl.ds(theirs, half), :].reshape(peer.shape)


def forward_body(side_ref, ro_ref, rp_ref, w2_ref, w3_ref, own_ref, peer_ref, mixed, narrow):
    side = side_ref[0]
    gather_rows(mixed, side, ro_ref, rp_ref)
    pre = mm(w2_ref[0], mixed[...], ((0,), (0,)))
    act = (0.5 * pre * (1.0 + jnp.tanh(GELU_A * (pre + GELU_B * (pre * pre * pre))))).astype(BF)
    narrow[...] = mm(w3_ref[0], act, ((0,), (0,))).astype(BF)
    split_rows(narrow, side, own_ref, peer_ref)


def plane_spec(array, plane, tile, start=0):
    peers, _, _, sub, _ = array.shape
    return pl.BlockSpec((peers, 1, 1, sub, tile), lambda c, i, s: (0, plane, start + c, 0, i))


def forward(side, own, peer, second, third, tile):
    peers, _, local, sub, tokens = own[0].shape
    bsize = second.shape[1]
    weight = pl.BlockSpec((1, bsize, bsize), lambda c, i, s: (c, 0, 0))
    return pl.pallas_call(
        forward_body,
        grid_spec=pltpu.PrefetchScalarGridSpec(
            num_scalar_prefetch=1,
            grid=(local, tokens // tile),
            in_specs=[plane_spec(*own, tile), plane_spec(*peer, tile), weight, weight],
            out_specs=[pl.BlockSpec((peers, 1, sub, tile), lambda c, i, s: (0, c, 0, i))] * 2,
            scratch_shapes=[pltpu.VMEM((bsize, tile), BF), pltpu.VMEM((bsize, tile), BF)],
        ),
        out_shape=[jax.ShapeDtypeStruct((peers, local, sub, tokens), BF)] * 2,
        compiler_params=params(VMEM_MIB),
        cost_estimate=cost(
            4 * local * bsize * bsize * tokens, 4 * local * bsize * tokens, local * bsize * tokens
        ),
        name="forward",
    )(side, own[0], peer[0], second, third)


def backward_body(
    steps, side_ref, ro_ref, rp_ref, go_ref, gp_ref, w2_ref, w3_ref, *rest,
):
    outs, (mixed, gnar, gmix, acc2, acc3) = rest[-7 - steps : -5], rest[-5:]
    mp_ref, g_ref, mo_refs = outs[0], outs[1], outs[2:]
    side = side_ref[0]
    step = pl.program_id(1)
    gather_rows(mixed, side, ro_ref, rp_ref)
    gather_rows(gnar, side, go_ref, gp_ref)
    pre = mm(w2_ref[0], mixed[...], ((0,), (0,)))
    square = pre * pre
    th = jnp.tanh(GELU_A * (pre + GELU_B * (square * pre)))
    half = 0.5 * (1.0 + th)
    act = (pre * half).astype(BF)
    slope = half + (0.5 * GELU_A) * pre * (1.0 - th * th) * (1.0 + (3.0 * GELU_B) * square)
    grad_act = mm(w3_ref[0], gnar[...], ((1,), (0,)))
    grad_pre = (grad_act * slope).astype(BF)
    gmix[...] = mm(w2_ref[0], grad_pre, ((1,), (0,))).astype(BF)
    for i, mo_ref in enumerate(mo_refs):

        @pl.when(step == i)
        def _(mo_ref=mo_ref):
            split_rows(gmix, side, mo_ref, mp_ref)

    add3 = mm(act, gnar[...], ((1,), (1,)))
    add2 = mm(mixed[...], grad_pre, ((1,), (1,)))

    @pl.when(step == 0)
    def _():
        acc2[...] = add2
        acc3[...] = add3

    @pl.when(step > 0)
    def _():
        acc2[...] += add2
        acc3[...] += add3

    @pl.when(step == pl.num_programs(1) - 1)
    def _():
        g_ref[0, 0] = acc2[...].astype(BF)
        g_ref[1, 0] = acc3[...].astype(BF)


def backward(side, own, peer, grad_own, grad_peer, second, third, tile, start, count, into):
    peers, _, local, sub, tokens = own[0].shape
    bsize = second.shape[1]
    steps = tokens // tile
    pieces = [plane_spec(*each, tile, start) for each in (own, peer, grad_own, grad_peer)]
    piece = pl.BlockSpec((peers, 1, sub, tile), lambda c, i, s: (0, start + c, 0, i))
    part = pl.BlockSpec((peers, 1, sub, tile), lambda c, i, s: (0, start + c, 0, 0))
    weight = pl.BlockSpec((1, bsize, bsize), lambda c, i, s: (start + c, 0, 0))
    grad = pl.BlockSpec((2, 1, bsize, bsize), lambda c, i, s: (0, c, 0, 0))
    grads = jax.ShapeDtypeStruct((2, count, bsize, bsize), BF)
    extra = () if into is None else into
    return pl.pallas_call(
        functools.partial(backward_body, steps),
        grid_spec=pltpu.PrefetchScalarGridSpec(
            num_scalar_prefetch=1,
            grid=(count, tokens // tile),
            in_specs=pieces + [weight] * 2 + [pl.BlockSpec(memory_space=pl.ANY)] * len(extra),
            out_specs=[piece, grad] + [part] * steps,
            scratch_shapes=[pltpu.VMEM((bsize, tile), BF)] * 3
            + [pltpu.VMEM((bsize, bsize), F32)] * 2,
        ),
        out_shape=[jax.ShapeDtypeStruct((peers, local, sub, tokens), BF), grads]
        + [jax.ShapeDtypeStruct((peers, local, sub, tile), BF)] * steps,
        input_output_aliases={7 + i: (0 if i == 0 else 1 + i) for i in range(len(extra))},
        compiler_params=params(VMEM_MIB),
        cost_estimate=cost(
            10 * count * bsize * bsize * tokens, 6 * count * bsize * tokens, count * bsize * tokens
        ),
        name="backward",
    )(side, own[0], peer[0], grad_own[0], grad_peer[0], second, third, *extra)


def emit_body(add, s_ref, a_ref, *rest):
    prev_ref, out_ref = rest if add else (None, rest[0])
    value = mm(a_ref[...], s_ref[...].reshape(a_ref.shape[1], -1), ((1,), (0,))).T
    if add:
        value = value + prev_ref[...].astype(F32)
    out_ref[...] = value.astype(BF)


def emit(s, plane, a, prev, tile, start, tokens):
    width, rows = a.shape
    peers, _, each, _ = s.shape
    first = start // tile
    add = prev is not None
    wide = pl.BlockSpec((tile, width), lambda i: (i, 0))
    return pl.pallas_call(
        functools.partial(emit_body, add),
        grid=(tokens // tile,),
        in_specs=[
            pl.BlockSpec((peers, 1, each, tile), lambda i: (0, plane, 0, first + i)),
            pl.BlockSpec((width, rows), lambda i: (0, 0)),
        ]
        + ([wide] if add else []),
        out_specs=wide,
        out_shape=jax.ShapeDtypeStruct((tokens, width), BF),
        compiler_params=params(VMEM_MIB),
        cost_estimate=cost(2 * rows * width * tokens, 2 * tokens * (rows + 2 * width)),
        name="emit",
    )(*((s, a) + ((prev,) if add else ())))


def wgrad_body(swap, groups, expand, count, *refs):
    s_refs, (x_ref, g_ref, acc) = refs[:count], refs[count:]
    step = pl.program_id(0)
    rows, width = acc.shape
    wide = width // groups
    sub = groups * expand * 2
    cols = 2 * rows // sub

    for i in range(count):

        @pl.when(step == i)
        def _(i=i):
            more = mm(s_refs[i][...].reshape(rows, -1), x_ref[...], ((1,), (0,)))
            acc[...] = more if i == 0 else acc[...] + more

    @pl.when(step == count - 1)
    def _():
        key = hot_key((rows, cols) if swap else (cols, rows), 0 if swap else 1, sub)
        for g in range(groups):
            part = acc[:, g * wide : (g + 1) * wide].astype(BF)
            if swap:
                part = part.T
            picks = [one_hot(key, g, k, sub) for k in range(expand)]
            if swap:
                got = mm(part, jnp.concatenate(picks, axis=1), ((1,), (0,))).astype(BF)
            else:
                got = mm(jnp.concatenate(picks, axis=0), part, ((1,), (0,))).astype(BF)
            for k in range(expand):
                at = slice(k * cols, (k + 1) * cols)
                g_ref[g, k] = got[:, at] if swap else got[at]


def wgrad(s, x, groups, expand, swap):
    count = len(s)
    width = x.shape[1]
    tile = x.shape[0] // count
    peers, _, each, _ = s[0][0].shape
    rows = peers * each
    bsize = width // groups
    cols = rows // (groups * expand)
    grads = (groups, expand, bsize, cols) if swap else (groups, expand, cols, bsize)
    specs = [
        pl.BlockSpec((peers, 1, each, tile), lambda i, plane=plane, at=at: (0, plane, 0, at))
        for _, plane, at in s
    ]
    return pl.pallas_call(
        functools.partial(wgrad_body, swap, groups, expand, count),
        grid=(count,),
        in_specs=specs + [pl.BlockSpec((tile, width), lambda i: (i, 0))],
        out_specs=pl.BlockSpec(grads, lambda i: (0, 0, 0, 0)),
        scratch_shapes=[pltpu.VMEM((rows, width), F32)],
        out_shape=jax.ShapeDtypeStruct(grads, BF),
        compiler_params=params(VMEM_MIB),
        cost_estimate=cost(2 * rows * width * x.shape[0], 2 * x.shape[0] * (rows + width)),
        name="wgrad",
    )(*[array for array, _, _ in s], x)


def copied(value):
    return place(value, None, 0, 1)


def swapped(value, axes):
    count = lax.axis_size(axes)
    return lax.ppermute(value, axes, [(i, count - 1 - i) for i in range(count)])


def shifted(value, axis, steps):
    count = lax.axis_size(axis)
    leading, last = (max(0, -steps), min(count, count - steps))
    return lax.ppermute(value, axis, [(source, source + steps) for source in range(leading, last)])


def spread_out(value):
    return lax.all_to_all(value, YC, split_axis=0, concat_axis=0, tiled=True)


def behind(value, after):
    return value if after is None else lax.optimization_barrier((value, after))[0]


def halves(value, dim):
    size = value.shape[dim] // 2
    return lax.slice_in_dim(value, 0, size, axis=dim), lax.slice_in_dim(value, size, 2 * size, axis=dim)


def join_body(count, *refs):
    out_refs = refs[2 * count :]
    start = 0
    for n in range(count):
        size = refs[2 * n].shape[1]
        for which, out_ref in enumerate(out_refs):
            out_ref[start : start + size] = refs[2 * n][which].astype(F32) + refs[2 * n + 1][which].astype(F32)
        start += size


def join(pairs):
    arrays = [each for pair in pairs for each in pair]
    results = arrays[0].shape[0]
    rest = arrays[0].shape[2:]
    total = (sum(a.shape[1] for a, _ in pairs),) + rest
    return pl.pallas_call(
        functools.partial(join_body, len(pairs)),
        grid=(1,),
        in_specs=[pl.BlockSpec(each.shape, lambda i: (0, 0, 0, 0)) for each in arrays],
        out_specs=[pl.BlockSpec(total, lambda i: (0, 0, 0))] * results,
        out_shape=[jax.ShapeDtypeStruct(total, F32)] * results,
        compiler_params=params(VMEM_MIB),
        cost_estimate=cost(1, 1),
        name="join",
    )(*arrays)


def paired_body(side_ref, ma_ref, mb_ref, ta_ref, tb_ref, *rest):
    step = pl.program_id(0)
    out_ref = rest[0] if len(rest) == 1 else rest[2]

    @pl.when(step == 0)
    def _():
        out_ref[...] = ma_ref[...].astype(F32) + mb_ref[...].astype(F32)
        if len(rest) > 1:
            rest[3][...] = rest[0][...]

    @pl.when(step == 1)
    def _():
        out_ref[...] = ta_ref[...].astype(F32) + tb_ref[...].astype(F32)


def paired(side, mine, theirs, dim, value=None, into=None):
    shape = mine[0].shape
    whole = pl.BlockSpec(shape, lambda i, s: (0,) * len(shape))

    def where(i, s):
        half = jnp.where(i == 0, s[0], 1 - s[0])
        return tuple(half if n == dim else 0 for n in range(len(shape)))

    full = tuple(2 * size if n == dim else size for n, size in enumerate(shape))
    in_specs, out_specs = [whole] * 4, [pl.BlockSpec(shape, where)]
    out_shape, extra = [jax.ShapeDtypeStruct(full, F32)], ()
    if value is not None:
        extra = (value, into)
        last = into.shape[0] // value.shape[0] - 1
        in_specs += [pl.BlockSpec(value.shape, lambda i, s: (0, 0)), pl.BlockSpec(memory_space=pl.ANY)]
        out_specs.append(pl.BlockSpec(value.shape, lambda i, s: (last, 0)))
        out_shape.append(jax.ShapeDtypeStruct(into.shape, into.dtype))
    return pl.pallas_call(
        paired_body,
        grid_spec=pltpu.PrefetchScalarGridSpec(
            num_scalar_prefetch=1, grid=(2,), in_specs=in_specs, out_specs=out_specs
        ),
        out_shape=out_shape,
        input_output_aliases={6: 1} if extra else {},
        compiler_params=params(VMEM_MIB),
        cost_estimate=cost(1, 1),
        name="paired",
    )(side, *mine, *theirs, *extra)


def place_body(value_ref, *rest):
    rest[-1][...] = value_ref[...]


def place(value, into, at, count):
    rows, width = value.shape
    extra = () if into is None else (into,)
    return pl.pallas_call(
        place_body,
        grid=(1,),
        in_specs=[pl.BlockSpec((rows, width), lambda i: (0, 0))]
        + [pl.BlockSpec(memory_space=pl.ANY)] * len(extra),
        out_specs=pl.BlockSpec((rows, width), lambda i: (at, 0)),
        out_shape=jax.ShapeDtypeStruct((count * rows, width), value.dtype),
        input_output_aliases={1: 0} if extra else {},
        compiler_params=params(VMEM_MIB),
        cost_estimate=cost(1, 1),
        name="place",
    )(value, *extra)


def shards(inputs, upstream, factor_one, factor_two, factor_three, factor_four):
    x, u = inputs[0], upstream[0]
    first, second, third, fourth = factor_one[0], factor_two[0], factor_three[0], factor_four[0]
    groups, expand, bsize = first.shape[0], first.shape[1], first.shape[2]
    local = groups * expand
    tokens = x.shape[0]
    peers = lax.axis_size("y") * lax.axis_size("core")
    low_or_high = lax.axis_index("xlo")
    is_low = low_or_high == 0
    side = low_or_high.astype(jnp.int32).reshape(1)
    zero = jnp.zeros((1,), jnp.int32)
    half = tokens // 2
    tile = half

    low, high = halves(first, 3)
    first_peer = swapped(jnp.where(is_low, high, low), "xlo")
    x_peer = swapped(x, "xlo")
    low, high = halves(fourth, 2)
    fourth_side = jnp.where(is_low, high, low)
    early = half
    u_early = swapped(behind(u[:early], (x_peer, first_peer)), "xlo")
    u_late = swapped(behind(u[early:], u_early), "xlo")
    fourth_peer = swapped(behind(fourth_side, u_early), "xlo")
    u_peer = jnp.concatenate([u_early, u_late], axis=0)

    def inner(value, after=None):
        return spread_out(behind(value, after)).reshape(peers, -1, local, 2 * local, tokens)

    def outer(value, after):
        value = value.reshape(peers, -1, 2 * local * local, value.shape[-1])
        return spread_out(behind(value, after))

    l12, a1o, a4o = lift([x, u], [first, fourth], [True, False], side, peers, tile)
    y12 = inner(l12)
    l1p, a1p = lift([x_peer], [first_peer], [True], zero, peers, tile)
    y1p = inner(l1p, (y12, u_early))
    l2p, a4p = lift([u_peer], [fourth_peer], [False], zero, peers, tile)
    y2p = inner(l2p, y1p)
    a1o, a4o, a1p, a4p = a1o.T, a4o.T, a1p.T, a4p.T
    no, np_ = forward(behind(side, (a1o, a4o, a1p, a4p)), (y12, 0), (y1p, 0), second, third, half)
    y3p = outer(np_, y2p)
    args = ((y12, 0), (y1p, 0), (y12, 1), (y2p, 0), second, third, half)
    first_cut, second_cut = 3 * local // 8, local // 2
    mp, ga, mo1, mo2 = backward(side, *args, 0, first_cut, None)
    da = swapped(ga, "dp")
    mp, gb, mo1, mo2 = backward(side, *args, first_cut, second_cut - first_cut, (mp, mo1, mo2))
    mp, gc, mo1, mo2 = backward(side, *args, second_cut, local - second_cut, (mp, mo1, mo2))
    y3o = outer(no, (y3p, mp, da))
    out_p = emit(y3p, 0, a4p, None, half, 0, tokens)
    out_peer = swapped(out_p, "xlo")
    g4p = wgrad([(y3p, 0, 0), (y3p, 0, 1)], behind(u_peer, out_p), groups, expand, False)
    y4p = outer(mp, (y3o, g4p, out_peer))
    db = swapped(behind(gb, out_peer), "dp")
    dc = swapped(behind(gc, out_peer), "dp")
    t4x, t4d = swapped(behind(g4p, out_peer), "xlo"), swapped(behind(g4p, out_peer), ("dp", "xlo"))
    out_o = emit(y3o, 0, a4o, out_peer, half, 0, tokens)
    y_next = copied(shifted(out_o, "pipe", 1))
    g4o = wgrad([(y3o, 0, 0), (y3o, 0, 1)], behind(u, out_o), groups, expand, False)
    y4a = outer(mo1, (y4p, g4o, db, dc, t4x, t4d))
    grad_two, grad_three = join([(ga, da), (gb, db), (gc, dc)])
    in_p1 = emit(y4p, 0, a1p, None, half, 0, half)
    in_peer1 = swapped(behind(in_p1, out_peer), "xlo")
    in_p2 = emit(y4p, 0, a1p, None, half, half, half)
    in_peer2 = swapped(in_p2, "xlo")
    g1p = wgrad([(y4p, 0, 0), (y4p, 0, 1)], behind(x_peer, in_p2), groups, expand, True)
    d4o = swapped(g4o, "dp")
    y4b = outer(mo2, (y4a, g1p, y_next, d4o))
    in_a = emit(y4a, 0, a1o, behind(in_peer1, g1p), half, 0, half)
    dx1 = shifted(in_a, "pipe", -1)
    late = (in_peer2, in_a, grad_two, grad_three)
    t1x, t1d = swapped(behind(g1p, late), "xlo"), swapped(behind(g1p, late), ("dp", "xlo"))
    in_b = emit(y4b, 0, a1o, in_peer2, half, 0, half)
    dx2 = shifted(behind(in_b, dx1), "pipe", -1)
    dx_prev = place(dx1, None, 0, 2)
    g1o = wgrad(
        [(y4a, 0, 0), (y4b, 0, 0)],
        behind(x, in_b),
        groups, expand, True,
    )
    d1o = swapped(behind(g1o, (t1x, t1d)), "dp")
    (grad_four,) = paired(side, (g4o, d4o), (t4x, t4d), 2)
    mine = (behind(g1o, grad_four), d1o)
    grad_one, dx_prev = paired(side, mine, (t1x, t1d), 3, dx2, dx_prev)
    return (
        y_next[None], dx_prev[None], grad_one[None], grad_two[None], grad_three[None], grad_four[None],
    )


def solution(mesh):
    parts = mesh.shape["tensor"]
    devices = mesh.devices.reshape(mesh.shape["dp"], mesh.shape["pipe"], 2, parts // 4, 2)
    fine = Mesh(devices, ("dp", "pipe", "xlo", "y", "core"))
    wide = ("xlo", "y", "core")
    acts = P("pipe", "dp", wide)
    five = P("pipe", wide, None, None, None)
    four = P("pipe", wide, None, None)
    return jax.shard_map(
        shards,
        mesh=fine,
        in_specs=(acts, acts, five, four, four, five),
        out_specs=(acts, acts, five, four, four, five),
        check_vma=False,
    )
```
